128 devices in a mesh: row: 8 (over y, z_lo), col: 16 (over x, z_hi, core).
Axes of the slice: x: 4, y: 4, z: 4 (z_hi: 2, z_lo: 2; z = z_hi * 2 + z_lo), core: 2. Of those that a mesh axis runs over, the one named last changes fastest.
Arguments:
- tokens: bfloat16 [4096, 6144], P('row', 'col'), may hold values from -40 to 40
- ln_gain: float32 [6144], replicated, may hold values from 0.25 to 1.75
- w_qkv: bfloat16 [6144, 3, 4096], P('row', None, 'col'), may hold values from -0.078125 to 0.078125
- q_gain: float32 [128], replicated, may hold values from 0.1 to 1.9
- k_gain: float32 [128], replicated, may hold values from 0.1 to 1.9
- w_up: bfloat16 [6144, 12288], P('row', 'col'), may hold values from -0.078125 to 0.078125
- w_out: bfloat16 [4096, 6144], P('col', 'row'), may hold values from -0.5 to 0.5
- w_down: bfloat16 [12288, 6144], P('col', 'row'), may hold values from -0.078125 to 0.078125
Outputs:
- mixed: bfloat16 [4096, 6144], P('row', 'col')
The draws below stay inside these ranges and needn't reach their ends.
All inputs are finite; a program needn't handle non-finite values.
Results may differ from the reference program's by a relative error of at most 0.017.
Values may be sent and summed in bfloat16 or wider, within the bound.
No kernel may reach another device: no remote copies, remote signals or barrier semaphores. Data moves between devices by JAX's collectives and lax.ppermute only.
A program may use at most 128 MiB of HBM per device.

```python
import math
import jax
import jax.numpy as jnp
from jax import lax

D = 6144
HEADS = 32
HD = 128
FF = 12288
PATCHES = 256
TOKENS = 4096
N_COL = 16


def draw_tokens(key, part):
    base = jax.random.fold_in(key, 7)
    key_noise, key_column, key_token = jax.random.split(base, 3)
    position = jnp.arange(D, dtype=jnp.float32) / D
    col_scale = 0.25 * jnp.exp(jnp.log(8.0) * position + jax.random.uniform(key_column, (D,), jnp.float32, -0.5, 0.5))
    noise = jnp.clip(jax.random.normal(key_noise, (TOKENS, D), jnp.float32), -6.0, 6.0)
    row_scale = jnp.exp(jax.random.uniform(key_token, (TOKENS, 1), jnp.float32, -0.5, 0.5))
    return (noise * col_scale * row_scale).astype(jnp.bfloat16)


def spiked(entries, own_key, source, target, blocks, factor):
    owner, partner = [(jnp.arange(entries.shape[dim]) // (entries.shape[dim] // blocks)).reshape([-1 if axis == dim else 1 for axis in range(entries.ndim)]) for dim in (source, target)]
    chosen = jax.random.permutation(own_key, blocks)[partner]
    strong = (owner == chosen) | (owner == (partner + blocks // 2) % blocks)
    return jnp.where(strong, factor * entries, entries)


def shard_levels(rng, extent, pieces, least, top_value):
    gain, own = 1.0, jax.random.fold_in(rng, 6)
    for dim, blocks in pieces:
        draws = jnp.exp(jax.random.uniform(jax.random.fold_in(own, dim), (blocks,), jnp.float32, least / len(pieces), top_value / len(pieces)))
        gain = gain * jnp.repeat(draws, extent[dim] // blocks).reshape([-1 if axis == dim else 1 for axis in range(len(extent))])
    return gain


def scatter_about(own_key, dims, width, reach, shards=(), held_as=jnp.bfloat16):
    level = shard_levels(own_key, dims, shards, -0.22, 0.18) if shards else 1.0
    entries = jax.random.normal(own_key, dims, jnp.float32) * width * level
    return jnp.minimum(jnp.maximum(entries, -reach), reach).astype(held_as)


def gaussian_with(key, dims, spread, most, shards, heavy, held_as=jnp.bfloat16):
    result = spread * jax.random.normal(key, dims, jnp.float32)
    if shards:
        result = result * shard_levels(key, dims, shards, -0.22, 0.18)
    return jnp.clip(spiked(result, jax.random.fold_in(key, 3), *heavy), -most, most).astype(held_as)


def setup_inputs(seed: int = 0) -> dict:
    arg_keys = jax.random.split(jax.random.key(seed), 9)
    return {
        "tokens": draw_tokens(jax.random.fold_in(arg_keys[8], 71), 0),
        "ln_gain": jnp.clip(1.0 + 0.15 * jax.random.normal(arg_keys[1], (D,), jnp.float32), 0.25, 1.75),
        "w_qkv": scatter_about(arg_keys[2], (D, 3, HEADS * HD), D ** -0.5, 0.078125, ((0, 8), (2, 16))),
        "q_gain": jnp.clip(1.0 + 0.18 * jax.random.normal(arg_keys[3], (HD,), jnp.float32), 0.1, 1.9),
        "k_gain": jnp.clip(1.0 + 0.18 * jax.random.normal(arg_keys[4], (HD,), jnp.float32), 0.1, 1.9),
        "w_up": scatter_about(arg_keys[5], (D, FF), D ** -0.5, 0.078125, ((0, 8), (1, 16))),
        "w_out": scatter_about(arg_keys[6], (HEADS * HD, D), HD ** -0.5, 0.5, ((0, 16), (1, 8))),
        "w_down": gaussian_with(arg_keys[7], (FF, D), FF ** -0.5, 0.078125, ((0, 16), (1, 8)), (0, 1, 16, 2.0)),
    }


epsilon = 1e-06

def layer_norm(values_in, gain_vec):
    x_float = values_in.astype(jnp.float32)
    centre = lax.optimization_barrier(jnp.mean(x_float, axis=-1, keepdims=True))
    deviation = x_float - centre
    variance = lax.optimization_barrier(jnp.mean(deviation * deviation, axis=-1, keepdims=True))
    return deviation * lax.rsqrt(variance + epsilon) * gain_vec

def attend(projected, q_gain, k_gain):
    tok_count = projected.shape[0]
    frame_count = tok_count // PATCHES
    arranged = projected.reshape(frame_count, PATCHES, 3, -1, HD)
    queries = layer_norm(arranged[:, :, 0], q_gain).astype(jnp.bfloat16)
    key_vecs = layer_norm(arranged[:, :, 1], k_gain).astype(jnp.bfloat16)
    value_vecs = arranged[:, :, 2].astype(jnp.bfloat16)
    scores = jnp.einsum('fqhd,fkhd->fhqk', queries.astype(jnp.float32), key_vecs.astype(jnp.float32)) / math.sqrt(HD)
    exponent = jnp.exp(scores)
    attn_probs = (exponent / lax.optimization_barrier(jnp.sum(exponent, axis=-1, keepdims=True))).astype(jnp.bfloat16)
    attended = jnp.einsum('fhqk,fkhd->fqhd', attn_probs.astype(jnp.float32), value_vecs.astype(jnp.float32))
    return attended.astype(jnp.bfloat16).reshape(tok_count, -1)

def reference(tokens, ln_gain, w_qkv, q_gain, k_gain, w_up, w_out, w_down):
    normed = layer_norm(tokens, ln_gain).astype(jnp.bfloat16)
    projected = jnp.dot(normed, w_qkv.reshape(D, 3 * HEADS * HD), preferred_element_type=jnp.float32)
    attended = attend(projected, q_gain, k_gain)
    pre_act = jnp.dot(normed, w_up, preferred_element_type=jnp.float32)
    activated = jax.nn.gelu(pre_act, approximate=False).astype(jnp.bfloat16)
    attn_width = HEADS * HD // N_COL
    hidden_width = FF // N_COL
    summed = jnp.zeros((TOKENS, D), jnp.float32)
    for column in range(N_COL):
        term = jnp.dot(attended[:, column * attn_width:(column + 1) * attn_width], w_out[column * attn_width:(column + 1) * attn_width], preferred_element_type=jnp.float32)
        term = term + jnp.dot(activated[:, column * hidden_width:(column + 1) * hidden_width], w_down[column * hidden_width:(column + 1) * hidden_width], preferred_element_type=jnp.float32)
        summed = summed + lax.optimization_barrier(term.astype(jnp.bfloat16)).astype(jnp.float32)
    return (tokens.astype(jnp.float32) + summed).astype(jnp.bfloat16)
```

```python
import functools
import math

import jax
import jax.numpy as jnp
from jax import lax
from jax.experimental import pallas as pl
from jax.experimental.pallas import tpu as pltpu
from jax.sharding import Mesh, PartitionSpec as P

HD = 128
PATCHES = 256
EPS = 1e-06
AXES = ("y", "l", "x", "h", "c")
SIZES = {"y": 4, "l": 2, "x": 4, "h": 2, "c": 2}
VMEM_LIMIT = 40 << 20
OFFSETS = (1, 3, 2, 0)


def shift(value, axis, by):
    size = SIZES[axis]
    return lax.ppermute(value, axis, [(i, (i + by) % size) for i in range(size)])


def move_z(value, pairs):
    place = lambda z: (z & 1) * 2 + (z >> 1)
    return lax.ppermute(value, ("l", "h"), [(place(s), place(d)) for s, d in pairs])


def norm_rows(value, gain):
    centre = jnp.mean(value, axis=-1, keepdims=True)
    deviation = value - centre
    variance = jnp.mean(deviation * deviation, axis=-1, keepdims=True)
    return deviation * lax.rsqrt(variance + EPS) * gain


def project_kernel(index, *refs):
    own, other = refs[0:4], refs[4:8]
    w_ref, mine_ref, theirs_ref, acc_ref = refs[8:]
    step = pl.program_id(0)
    core, slot = index[4], index[5]
    groups, width = w_ref.shape[1], w_ref.shape[-1]
    for j in range(4):

        @pl.when(step == j)
        def _():
            for g in range(groups):
                part = jnp.dot(
                    own[j][...].reshape(1024, 384), w_ref[0, g, core], preferred_element_type=jnp.float32
                )
                part += jnp.dot(
                    other[j][...].reshape(1024, 384), w_ref[0, g, 1 - core], preferred_element_type=jnp.float32
                )
                part = part.reshape(2, 512, width)
                cols = slice(g * width, (g + 1) * width)
                if j:
                    part += acc_ref[:, :, cols]
                acc_ref[:, :, cols] = part

    @pl.when(step == 3)
    def _():
        mine_ref[...] = acc_ref[slot]
        theirs_ref[...] = acc_ref[1 - slot].astype(jnp.bfloat16)


def project(index, own, other, weights):
    groups, width = weights.shape[1], weights.shape[-1]
    total = groups * width
    piece = pl.BlockSpec((2, 512, 384), lambda j, i: (0, 0, 0))
    whole = pl.BlockSpec((512, total), lambda j, i: (0, 0))
    return pl.pallas_call(
        project_kernel,
        out_shape=(
            jax.ShapeDtypeStruct((512, total), jnp.float32),
            jax.ShapeDtypeStruct((512, total), jnp.bfloat16),
        ),
        grid_spec=pltpu.PrefetchScalarGridSpec(
            num_scalar_prefetch=1,
            grid=(4,),
            in_specs=[piece] * 8
            + [pl.BlockSpec((1, groups, 2, 384, width), lambda j, i: (i[j], 0, 0, 0, 0))],
            out_specs=(whole, whole),
            scratch_shapes=[pltpu.VMEM((2, 512, total), jnp.float32)],
        ),
        compiler_params=pltpu.CompilerParams(vmem_limit_bytes=VMEM_LIMIT),
        cost_estimate=pl.CostEstimate(
            flops=2 * 1024 * 3072 * total, bytes_accessed=2 * 3072 * (1024 + total), transcendentals=0
        ),
    )(index, *own, *other, weights)


def attend_kernel(mine_ref, got_ref, q_gain_ref, k_gain_ref, out_ref):
    for frame in range(2):
        rows = slice(frame * PATCHES, (frame + 1) * PATCHES)
        for head in range(2):

            def part(which):
                cols = slice(which * 256 + head * HD, which * 256 + (head + 1) * HD)
                return mine_ref[rows, cols] + got_ref[rows, cols].astype(jnp.float32)

            queries = norm_rows(part(0), q_gain_ref[...]).astype(jnp.bfloat16)
            key_vecs = norm_rows(part(1), k_gain_ref[...]).astype(jnp.bfloat16)
            scores = lax.dot_general(
                queries, key_vecs, (((1,), (1,)), ((), ())), preferred_element_type=jnp.float32
            ) / math.sqrt(HD)
            exponent = jnp.exp(scores)
            probs = (exponent / jnp.sum(exponent, axis=-1, keepdims=True)).astype(jnp.bfloat16)
            out_ref[rows, head * HD : (head + 1) * HD] = jnp.dot(
                probs, part(2).astype(jnp.bfloat16), preferred_element_type=jnp.float32
            ).astype(jnp.bfloat16)


def attend(mine, got, q_gain, k_gain):
    return pl.pallas_call(
        attend_kernel,
        out_shape=jax.ShapeDtypeStruct((512, 256), jnp.bfloat16),
        compiler_params=pltpu.CompilerParams(vmem_limit_bytes=VMEM_LIMIT),
        cost_estimate=pl.CostEstimate(
            flops=4 * 4 * 256 * 256 * 128, bytes_accessed=512 * 768 * 6, transcendentals=4 * 256 * 256
        ),
    )(mine, got, q_gain.reshape(1, HD), k_gain.reshape(1, HD))


def output_kernel(index, att_own, att_other, act_own, act_other, w_out_ref, w_down_ref, *outs):
    keep, send = outs[0:4], outs[4:8]
    step = pl.program_id(0)
    core, slot = index[4], index[5]
    for j in range(4):

        @pl.when(step == j)
        def _():
            for att, act, place in ((att_own, act_own, slot), (att_other, act_other, 1 - slot)):
                for half, target in ((core, keep[j]), (1 - core, send[j])):
                    cols = pl.ds(pl.multiple_of(half * 384, 128), 384)
                    term = jnp.dot(att[...], w_out_ref[0, :, cols], preferred_element_type=jnp.float32)
                    term += jnp.dot(act[...], w_down_ref[0, :, cols], preferred_element_type=jnp.float32)
                    target[place] = term.astype(jnp.bfloat16)


def output_terms(index, att_own, att_other, act_own, act_other, w_out, w_down):
    whole = lambda *shape: pl.BlockSpec(shape, lambda j, i: (0,) * len(shape))
    return pl.pallas_call(
        output_kernel,
        out_shape=[jax.ShapeDtypeStruct((2, 512, 384), jnp.bfloat16)] * 8,
        grid_spec=pltpu.PrefetchScalarGridSpec(
            num_scalar_prefetch=1,
            grid=(4,),
            in_specs=[whole(512, 256), whole(512, 256), whole(512, 768), whole(512, 768)]
            + [pl.BlockSpec((1, k, 768), lambda j, i: (i[j], 0, 0)) for k in (256, 768)],
            out_specs=[whole(2, 512, 384)] * 8,
        ),
        compiler_params=pltpu.CompilerParams(vmem_limit_bytes=VMEM_LIMIT),
        cost_estimate=pl.CostEstimate(
            flops=2 * 1024 * 1024 * 3072, bytes_accessed=2 * 3072 * 2048, transcendentals=0
        ),
    )(index, att_own, att_other, act_own, act_other, w_out, w_down)


def shards(tokens, ln_gain, w_qkv, q_gain, k_gain, w_up, w_out, w_down):
    x, h, l, c = (lax.axis_index(a) for a in ("x", "h", "l", "c"))
    slot = jnp.where(l == h, 1, 0)
    index = jnp.stack([(x + o) % 4 for o in OFFSETS] + [c, slot]).astype(jnp.int32)

    qkv_all = lax.all_gather(w_qkv.transpose(1, 0, 2).reshape(3, 2, 384, 256), "y", axis=0)
    up_all = lax.all_gather(w_up.reshape(1, 2, 384, 768), "y", axis=0)
    out_all = lax.all_gather(w_out, "y", axis=0)
    down_all = lax.all_gather(w_down, "y", axis=0)

    local = tokens.astype(jnp.float32)
    mean = jnp.mean(local, axis=-1)
    deviation = local - mean[:, None]
    square = jnp.sum(deviation * deviation, axis=-1)
    stats = lax.all_gather(jnp.stack([mean, square]), ("x", "h", "c"), axis=0)
    centre = jnp.mean(stats[:, 0], axis=0)
    spread = jnp.sum(stats[:, 1] + 384 * (stats[:, 0] - centre) ** 2, axis=0) / 6144
    gain = lax.dynamic_slice(ln_gain, ((x * 4 + h * 2 + c) * 384,), (384,))
    normed = ((local - centre[:, None]) * lax.rsqrt(spread + EPS)[:, None] * gain).astype(jnp.bfloat16)

    block_a = move_z(normed, [(1, 0), (0, 2), (3, 1), (2, 3)])
    block_b = move_z(normed, [(0, 0), (1, 2), (2, 1), (3, 3)])
    held = jnp.stack([block_a, block_b])
    own = [shift(held, "x", -o) if o else held for o in OFFSETS]
    other = [shift(piece, "c", 1) for piece in own]

    qkv_mine, qkv_theirs = project(index, own, other, qkv_all)
    attended = attend(qkv_mine, shift(qkv_theirs, "l", 1), q_gain, k_gain)
    attended_other = shift(attended, "l", 1)

    up_mine, up_theirs = project(index, own, other, up_all)
    pre_act = up_mine + shift(up_theirs, "l", 1).astype(jnp.float32)
    activated = jax.nn.gelu(pre_act, approximate=False).astype(jnp.bfloat16)
    activated_other = shift(activated, "l", 1)

    outs = output_terms(index, attended, attended_other, activated, activated_other, out_all, down_all)
    summed = 0.0
    for j, o in enumerate(OFFSETS):
        pair = outs[j].astype(jnp.float32) + shift(outs[4 + j], "c", 1).astype(jnp.float32)
        if o:
            pair = shift(pair.astype(jnp.bfloat16), "x", o).astype(jnp.float32)
        summed = summed + pair
    block_a, block_b = summed[0].astype(jnp.bfloat16), summed[1].astype(jnp.bfloat16)
    got_a = move_z(block_a, [(0, 1), (2, 0), (1, 3), (3, 2)])
    got_b = move_z(block_b, [(0, 0), (2, 1), (1, 2), (3, 3)])
    return (local + got_a.astype(jnp.float32) + got_b.astype(jnp.float32)).astype(jnp.bfloat16)


def solution(mesh):
    fine = Mesh(mesh.devices.reshape(4, 2, 4, 2, 2), AXES)
    row, col = ("y", "l"), ("x", "h", "c")
    in_specs = (
        P(row, col),
        P(),
        P(row, None, col),
        P(),
        P(),
        P(row, col),
        P(col, row),
        P(col, row),
    )
    return jax.shard_map(shards, mesh=fine, in_specs=in_specs, out_specs=P(row, col), check_vma=False)
```

```python
import functools
import math

import jax
import jax.numpy as jnp
from jax import lax
from jax.experimental import pallas as pl
from jax.experimental.pallas import tpu as pltpu
from jax.sharding import Mesh, PartitionSpec as P

HD = 128
PATCHES = 256
EPS = 1e-06
AXES = ("y", "l", "x", "h", "c")
SIZES = {"y": 4, "l": 2, "x": 4, "h": 2, "c": 2}
VMEM_LIMIT = 56 << 20
STEPS = (0, 1, 3, 2)
ROWS = 768


def shift(value, axis, by):
    size = SIZES[axis]
    return lax.ppermute(value, axis, [(i, (i + by) % size) for i in range(size)])


def move_z(value, pairs):
    place = lambda z: (z & 1) * 2 + (z >> 1)
    return lax.ppermute(value, ("l", "h"), [(place(s), place(d)) for s, d in pairs])


def norm_rows(value, gain):
    centre = jnp.mean(value, axis=-1, keepdims=True)
    deviation = value - centre
    variance = jnp.mean(deviation * deviation, axis=-1, keepdims=True)
    return deviation * lax.rsqrt(variance + EPS) * gain


def project_kernel(index, *refs):
    own, other, (centre, scale, gain, w_ref) = refs[0:5], refs[5:10], refs[10:14]
    sum_ref, sent_ref, block_ref = refs[14:]
    step, core = pl.program_id(0), index[2]
    for j in range(4):

        @pl.when(step == j)
        def _():
            for pieces, place in ((own, core), (other, 1 - core)):
                for t in range(2):
                    raw = pieces[3 + t][...] if j == 3 else pieces[j][t]
                    value = (raw.astype(jnp.float32) - centre[t]) * scale[t] * gain[0, 0, place]
                    block_ref[0, place, t * 512 : (t + 1) * 512] = value.astype(jnp.bfloat16)

    multiply(step, block_ref, w_ref, sum_ref)

    @pl.when(step == 3)
    def _():
        sent_ref[...] = sum_ref[...].astype(jnp.bfloat16)


def project_again_kernel(index, block_ref, w_ref, mine_ref, theirs_ref, acc_ref):
    step = pl.program_id(0)
    multiply(step, block_ref, w_ref, acc_ref)
    finish(step, index, acc_ref, mine_ref, theirs_ref)


def multiply(step, block_ref, w_ref, acc_ref):
    groups, width = w_ref.shape[1], w_ref.shape[-1]

    @pl.when(step == 0)
    def _():
        acc_ref[...] = jnp.zeros_like(acc_ref)

    for g in range(groups):
        cols = slice(g * width, (g + 1) * width)
        part = jnp.dot(block_ref[0, 0], w_ref[0, g, :384], preferred_element_type=jnp.float32)
        part += jnp.dot(block_ref[0, 1], w_ref[0, g, 384:], preferred_element_type=jnp.float32)
        acc_ref[:, :, cols] += part.reshape(2, 512, width)


def finish(step, index, acc_ref, mine_ref, theirs_ref):
    @pl.when(step == 3)
    def _():
        slot = index[1]
        mine_ref[...] = acc_ref[slot]
        theirs_ref[...] = acc_ref[1 - slot].astype(jnp.bfloat16)


def call(kernel, index, arrays, specs, outs, out_specs, scratch, flops):
    size = lambda a: math.prod(a.shape) * a.dtype.itemsize
    whole = lambda a: pl.BlockSpec(a.shape, lambda j, i, n=len(a.shape): (0,) * n)
    return pl.pallas_call(
        kernel,
        out_shape=outs,
        grid_spec=pltpu.PrefetchScalarGridSpec(
            num_scalar_prefetch=1,
            grid=(4,),
            in_specs=[spec or whole(a) for a, spec in zip(arrays, specs)],
            out_specs=[spec or whole(a) for a, spec in zip(outs, out_specs)],
            scratch_shapes=scratch,
        ),
        compiler_params=pltpu.CompilerParams(vmem_limit_bytes=VMEM_LIMIT),
        cost_estimate=pl.CostEstimate(
            flops=flops,
            bytes_accessed=sum(map(size, arrays)) + sum(map(size, outs)),
            transcendentals=0,
        ),
    )(index, *arrays)


def order(j):
    return j + (j == 2) * 1 - (j == 3) * 1


def by_block(which, *shape):
    return pl.BlockSpec((1, *shape), lambda j, i: ((i[which] + order(j)) % 4,) + (0,) * len(shape))


PARTS = [jax.ShapeDtypeStruct((512, ROWS), t) for t in (jnp.float32, jnp.bfloat16)]
SUMS = [pltpu.VMEM((2, 512, ROWS), jnp.float32)]
BY_STEP = pl.BlockSpec((1, 2, 1024, 384), lambda j, i: (j, 0, 0, 0))


def project(index, own, other, centre, scale, gain, weights):
    return call(
        project_kernel,
        index,
        [*own, *other, centre, scale, gain, weights],
        [None] * 12
        + [pl.BlockSpec((1, 1, 2, 1, 384), lambda j, i: ((i[3] + order(j)) % 4, i[5], 0, 0, 0))]
        + [by_block(3, *weights.shape[1:])],
        [
            jax.ShapeDtypeStruct((2, 512, ROWS), jnp.float32),
            jax.ShapeDtypeStruct((2, 512, ROWS), jnp.bfloat16),
            jax.ShapeDtypeStruct((4, 2, 1024, 384), jnp.bfloat16),
        ],
        [None, None, BY_STEP],
        [],
        2 * 1024 * 3072 * ROWS,
    )


def project_again(index, features, weights):
    return call(
        project_again_kernel,
        index,
        [features, weights],
        [BY_STEP, by_block(3, *weights.shape[1:])],
        PARTS,
        [None, None],
        SUMS,
        2 * 1024 * 3072 * ROWS,
    )


def attend_kernel(mine_ref, got_ref, q_gain_ref, k_gain_ref, out_ref):
    for frame in range(2):
        rows = slice(frame * PATCHES, (frame + 1) * PATCHES)
        for head in range(2):

            def part(which):
                cols = slice(which * 256 + head * HD, which * 256 + (head + 1) * HD)
                return mine_ref[rows, cols] + got_ref[rows, cols].astype(jnp.float32)

            queries = norm_rows(part(0), q_gain_ref[...]).astype(jnp.bfloat16)
            key_vecs = norm_rows(part(1), k_gain_ref[...]).astype(jnp.bfloat16)
            scores = lax.dot_general(
                queries, key_vecs, (((1,), (1,)), ((), ())), preferred_element_type=jnp.float32
            ) / math.sqrt(HD)
            exponent = jnp.exp(scores)
            probs = (exponent / jnp.sum(exponent, axis=-1, keepdims=True)).astype(jnp.bfloat16)
            out_ref[rows, head * HD : (head + 1) * HD] = jnp.dot(
                probs, part(2).astype(jnp.bfloat16), preferred_element_type=jnp.float32
            ).astype(jnp.bfloat16)


def attend(mine, got, q_gain, k_gain):
    return pl.pallas_call(
        attend_kernel,
        out_shape=jax.ShapeDtypeStruct((512, 256), jnp.bfloat16),
        compiler_params=pltpu.CompilerParams(vmem_limit_bytes=VMEM_LIMIT),
        cost_estimate=pl.CostEstimate(
            flops=4 * 4 * 256 * 256 * 128, bytes_accessed=512 * 768 * 6, transcendentals=4 * 256 * 256
        ),
    )(mine, got, q_gain.reshape(1, HD), k_gain.reshape(1, HD))


def output_kernel(block, index, att_own, att_other, act_ref, w_out_ref, *refs):
    pieces, (keep_ref, send_ref) = refs[:5], refs[5:]
    step, first = pl.program_id(0), index[2] == 0

    def terms(*rows):
        att = jnp.where(index[1] == block, att_own[...], att_other[...])
        term = jnp.dot(att, w_out_ref[0], preferred_element_type=jnp.float32)
        start = 0
        for right in rows:
            stop = start + right.shape[0]
            term += jnp.dot(act_ref[0, :, start:stop], right[...], preferred_element_type=jnp.float32)
            start = stop
        term = term.astype(jnp.bfloat16)
        keep_ref[0] = jnp.where(first, term[:, :384], term[:, 384:])
        send_ref[0] = jnp.where(first, term[:, 384:], term[:, :384])

    for j in range(4):
        pl.when(step == j)(lambda: terms(*(pieces[3:] if j == 3 else [pieces[j]])))


def output_terms(index, block, att_own, att_other, activated, w_out, w_down):
    out = jax.ShapeDtypeStruct((4, 512, 384), jnp.bfloat16)
    out_spec = pl.BlockSpec((1, 512, 384), lambda j, i: ((i[4] + order(j)) % 4, 0, 0))
    return call(
        functools.partial(output_kernel, block),
        index,
        [att_own, att_other, activated, w_out, *w_down],
        [None, None, pl.BlockSpec((1, 512, ROWS), lambda j, i: (block, 0, 0)), by_block(0, 256, ROWS)]
        + [None] * 5,
        [out, out],
        [out_spec, out_spec],
        [],
        2 * 512 * 1024 * 4 * ROWS,
    )


def after(value, *others):
    return lax.optimization_barrier((value, *others))[0]


def ring(block, axis, halves, ready=lambda *v: v):
    after, before = ready(shift(block, axis, -1), shift(block, axis, 1))
    return block, after, before, shift(halves(before)[0], axis, 1), shift(halves(after)[1], axis, -1)


def moments(piece):
    value = piece.astype(jnp.float32)
    mean = jnp.mean(value, axis=-1)
    return mean, jnp.sum((value - mean[..., None]) ** 2, axis=-1)


def merge(stats, count):
    means = [s[0] for s in stats]
    centre = 0.25 * (means[0] + means[1] + means[2] + means[3])
    total = stats[0][1] + stats[1][1] + stats[2][1] + stats[3][1]
    for m in means:
        total = total + count * (m - centre) ** 2
    return centre, total


def shards(tokens, ln_gain, w_qkv, q_gain, k_gain, w_up, w_out, w_down):
    y, x, h, l, c = (lax.axis_index(a) for a in ("y", "x", "h", "l", "c"))
    slot = jnp.where(l == h, 1, 0)
    index = jnp.stack([y, slot, c, x, (y - x + 4) % 4, l]).astype(jnp.int32)

    up_all = lax.all_gather(w_up[None], "y", axis=0)
    qkv_all = lax.all_gather(w_qkv.transpose(1, 0, 2), "y", axis=0)

    block_a = move_z(tokens, [(1, 0), (0, 2), (3, 1), (2, 3)])
    block_b = move_z(tokens, [(0, 0), (1, 2), (2, 1), (3, 3)])
    own = ring(jnp.stack([block_a, block_b]), "x", lambda v: (v[0], v[1]))
    other = [shift(piece, "c", 1) for piece in own]

    parts = [moments(piece) for piece in own]
    last = [jnp.stack([a, b]) for a, b in zip(parts[3], parts[4])]
    stats = jnp.stack(merge([*parts[:3], last], 384))
    cross = lax.ppermute(stats, ("l", "c"), [(i, 3 - i) for i in range(4)])
    centre, spread = merge([stats, shift(stats, "c", 1), shift(stats, "l", 1), cross], 1536)
    centre, scale = lax.optimization_barrier((centre, lax.rsqrt(spread / 6144 + EPS)))
    gain = ln_gain.reshape(4, 2, 2, 1, 384)

    up_sum, up_sent, features = project(
        index, own, other, centre[..., None], scale[..., None], gain, up_all
    )
    pre_act = up_sum + shift(up_sent, "l", 1).astype(jnp.float32)
    activated = jax.nn.gelu(pre_act, approximate=False).astype(jnp.bfloat16)

    qkv_mine, qkv_theirs = project_again(index, features, qkv_all)

    out_all = lax.all_gather(after(w_out, qkv_all), "y", axis=0)
    w_down = after(w_down, qkv_all)
    after_w, before_w = shift(w_down, "y", -1), shift(w_down, "y", 1)
    forward = before_w[:384], after_w[384:]
    down = w_down, after_w, before_w, shift(forward[0], "y", 1), shift(forward[1], "y", -1)

    got = after(shift(qkv_theirs, "l", 1), activated, *forward)
    attended = attend(qkv_mine, got, q_gain, k_gain)
    attended_other = shift(attended, "l", 1)

    def start_terms(block):
        keep, send = output_terms(
            index, block, attended, attended_other, activated, out_all, down
        )
        return keep, shift(send, "c", 1)

    def start_sums(keep, got):
        pair = [keep[o].astype(jnp.float32) + got[o].astype(jnp.float32) for o in range(4)]
        return pair[0], [shift(pair[o].astype(jnp.bfloat16), "x", o) for o in (2, 1, 3)]

    def finish_sums(summed, got, pairs):
        for g in got:
            summed = summed + g.astype(jnp.float32)
        return move_z(summed.astype(jnp.bfloat16), pairs).astype(jnp.float32)

    keep_a, got_a = start_terms(0)
    keep_b, got_b = start_terms(1)
    sum_a, sent_a = start_sums(keep_a, got_a)
    sum_b, sent_b = start_sums(keep_b, got_b)
    part_a = finish_sums(sum_a, sent_a, [(0, 1), (2, 0), (1, 3), (3, 2)])
    part_b = finish_sums(sum_b, sent_b, [(0, 0), (2, 1), (1, 2), (3, 3)])
    return (tokens.astype(jnp.float32) + part_a + part_b).astype(jnp.bfloat16)


def solution(mesh):
    fine = Mesh(mesh.devices.reshape(4, 2, 4, 2, 2), AXES)
    row, col = ("y", "l"), ("x", "h", "c")
    in_specs = (
        P(row, col),
        P(),
        P(row, None, col),
        P(),
        P(),
        P(row, col),
        P(col, row),
        P(col, row),
    )
    return jax.shard_map(shards, mesh=fine, in_specs=in_specs, out_specs=P(row, col), check_vma=False)
```

```python
import functools
import math

import jax
import jax.numpy as jnp
from jax import lax
from jax.experimental import pallas as pl
from jax.experimental.pallas import tpu as pltpu
from jax.sharding import Mesh, PartitionSpec as P

HD = 128
PATCHES = 256
EPS = 1e-06
AXES = ("y", "l", "x", "h", "c")
SIZES = {"y": 4, "l": 2, "x": 4, "h": 2, "c": 2}
VMEM_LIMIT = 56 << 20
STEPS = (0, 1, 3, 2)
ROWS = 768


def shift(value, axis, by):
    size = SIZES[axis]
    return lax.ppermute(value, axis, [(i, (i + by) % size) for i in range(size)])


def move_z(value, pairs):
    place = lambda z: (z & 1) * 2 + (z >> 1)
    return lax.ppermute(value, ("l", "h"), [(place(s), place(d)) for s, d in pairs])


def norm_rows(value, gain):
    centre = jnp.mean(value, axis=-1, keepdims=True)
    deviation = value - centre
    variance = jnp.mean(deviation * deviation, axis=-1, keepdims=True)
    return deviation * lax.rsqrt(variance + EPS) * gain


def project_kernel(index, *refs):
    own, other, (centre, scale, gain, w_ref) = refs[0:5], refs[5:10], refs[10:14]
    sum_ref, sent_ref, block_ref = refs[14:]
    step, core = pl.program_id(0), index[2]
    for j in range(4):

        @pl.when(step == j)
        def _():
            for pieces, place in ((own, core), (other, 1 - core)):
                for t in range(2):
                    raw = pieces[3 + t][...] if j == 3 else pieces[j][t]
                    value = (raw.astype(jnp.float32) - centre[t]) * scale[t] * gain[0, 0, place]
                    block_ref[0, place, t * 512 : (t + 1) * 512] = value.astype(jnp.bfloat16)

    multiply(step, block_ref, w_ref, sum_ref)

    @pl.when(step == 3)
    def _():
        sent_ref[...] = sum_ref[...].astype(jnp.bfloat16)


def project_again_kernel(index, block_ref, w_ref, mine_ref, theirs_ref, acc_ref):
    step = pl.program_id(0)
    multiply(step, block_ref, w_ref, acc_ref)
    finish(step, index, acc_ref, mine_ref, theirs_ref)


def multiply(step, block_ref, w_ref, acc_ref):
    groups, width = w_ref.shape[1], w_ref.shape[-1]

    @pl.when(step == 0)
    def _():
        acc_ref[...] = jnp.zeros_like(acc_ref)

    for g in range(groups):
        cols = slice(g * width, (g + 1) * width)
        part = jnp.dot(block_ref[0, 0], w_ref[0, g, :384], preferred_element_type=jnp.float32)
        part += jnp.dot(block_ref[0, 1], w_ref[0, g, 384:], preferred_element_type=jnp.float32)
        acc_ref[:, :, cols] += part.reshape(2, 512, width)


def finish(step, index, acc_ref, mine_ref, theirs_ref):
    @pl.when(step == 3)
    def _():
        slot = index[1]
        mine_ref[...] = acc_ref[slot]
        theirs_ref[...] = acc_ref[1 - slot].astype(jnp.bfloat16)


def call(kernel, index, arrays, specs, outs, out_specs, scratch, flops):
    size = lambda a: math.prod(a.shape) * a.dtype.itemsize
    whole = lambda a: pl.BlockSpec(a.shape, lambda j, i, n=len(a.shape): (0,) * n)
    return pl.pallas_call(
        kernel,
        out_shape=outs,
        grid_spec=pltpu.PrefetchScalarGridSpec(
            num_scalar_prefetch=1,
            grid=(4,),
            in_specs=[spec or whole(a) for a, spec in zip(arrays, specs)],
            out_specs=[spec or whole(a) for a, spec in zip(outs, out_specs)],
            scratch_shapes=scratch,
        ),
        compiler_params=pltpu.CompilerParams(vmem_limit_bytes=VMEM_LIMIT),
        cost_estimate=pl.CostEstimate(
            flops=flops,
            bytes_accessed=sum(map(size, arrays)) + sum(map(size, outs)),
            transcendentals=0,
        ),
    )(index, *arrays)


def order(j):
    return j + (j == 2) * 1 - (j == 3) * 1


def by_block(which, *shape):
    return pl.BlockSpec((1, *shape), lambda j, i: ((i[which] + order(j)) % 4,) + (0,) * len(shape))


PARTS = [jax.ShapeDtypeStruct((512, ROWS), t) for t in (jnp.float32, jnp.bfloat16)]
SUMS = [pltpu.VMEM((2, 512, ROWS), jnp.float32)]
BY_STEP = pl.BlockSpec((1, 2, 1024, 384), lambda j, i: (j, 0, 0, 0))


def project(index, own, other, centre, scale, gain, weights):
    return call(
        project_kernel,
        index,
        [*own, *other, centre, scale, gain, weights],
        [None] * 12
        + [pl.BlockSpec((1, 1, 2, 1, 384), lambda j, i: ((i[3] + order(j)) % 4, i[5], 0, 0, 0))]
        + [by_block(3, *weights.shape[1:])],
        [
            jax.ShapeDtypeStruct((2, 512, ROWS), jnp.float32),
            jax.ShapeDtypeStruct((2, 512, ROWS), jnp.bfloat16),
            jax.ShapeDtypeStruct((4, 2, 1024, 384), jnp.bfloat16),
        ],
        [None, None, BY_STEP],
        [],
        2 * 1024 * 3072 * ROWS,
    )


def project_again(index, features, weights):
    return call(
        project_again_kernel,
        index,
        [features, weights],
        [BY_STEP, by_block(3, *weights.shape[1:])],
        PARTS,
        [None, None],
        SUMS,
        2 * 1024 * 3072 * ROWS,
    )


def attend_kernel(mine_ref, got_ref, q_gain_ref, k_gain_ref, out_ref):
    for frame in range(2):
        rows = slice(frame * PATCHES, (frame + 1) * PATCHES)
        for head in range(2):

            def part(which):
                cols = slice(which * 256 + head * HD, which * 256 + (head + 1) * HD)
                return mine_ref[rows, cols] + got_ref[rows, cols].astype(jnp.float32)

            queries = norm_rows(part(0), q_gain_ref[...]).astype(jnp.bfloat16)
            key_vecs = norm_rows(part(1), k_gain_ref[...]).astype(jnp.bfloat16)
            scores = lax.dot_general(
                queries, key_vecs, (((1,), (1,)), ((), ())), preferred_element_type=jnp.float32
            ) / math.sqrt(HD)
            exponent = jnp.exp(scores)
            probs = (exponent / jnp.sum(exponent, axis=-1, keepdims=True)).astype(jnp.bfloat16)
            out_ref[rows, head * HD : (head + 1) * HD] = jnp.dot(
                probs, part(2).astype(jnp.bfloat16), preferred_element_type=jnp.float32
            ).astype(jnp.bfloat16)


def attend(mine, got, q_gain, k_gain):
    return pl.pallas_call(
        attend_kernel,
        out_shape=jax.ShapeDtypeStruct((512, 256), jnp.bfloat16),
        compiler_params=pltpu.CompilerParams(vmem_limit_bytes=VMEM_LIMIT),
        cost_estimate=pl.CostEstimate(
            flops=4 * 4 * 256 * 256 * 128, bytes_accessed=512 * 768 * 6, transcendentals=4 * 256 * 256
        ),
    )(mine, got, q_gain.reshape(1, HD), k_gain.reshape(1, HD))


def output_kernel(block, index, att_own, att_other, act_ref, *refs):
    w_out, w_down, (keep_ref, send_ref) = refs[:4], refs[4:9], refs[9:]
    step, first = pl.program_id(0), index[2] == 0

    def terms(w_att, *w_act):
        att = jnp.where(index[1] == block, att_own[...], att_other[...])
        term = jnp.dot(att, w_att[...], preferred_element_type=jnp.float32)
        start = 0
        for right in w_act:
            stop = start + right.shape[0]
            term += jnp.dot(act_ref[0, :, start:stop], right[...], preferred_element_type=jnp.float32)
            start = stop
        term = term.astype(jnp.bfloat16)
        keep_ref[0] = jnp.where(first, term[:, :384], term[:, 384:])
        send_ref[0] = jnp.where(first, term[:, 384:], term[:, :384])

    for j in range(4):
        pl.when(step == j)(lambda: terms(w_out[j], *(w_down[3:] if j == 3 else [w_down[j]])))


def output_terms(index, block, att_own, att_other, activated, w_out, w_down):
    out = jax.ShapeDtypeStruct((4, 512, 384), jnp.bfloat16)
    out_spec = pl.BlockSpec((1, 512, 384), lambda j, i: ((i[4] + order(j)) % 4, 0, 0))
    return call(
        functools.partial(output_kernel, block),
        index,
        [att_own, att_other, activated, *w_out, *w_down],
        [None, None, pl.BlockSpec((1, 512, ROWS), lambda j, i: (block, 0, 0))] + [None] * 9,
        [out, out],
        [out_spec, out_spec],
        [],
        2 * 512 * 1024 * 4 * ROWS,
    )


def after(value, *others):
    return lax.optimization_barrier((value, *others))[0]


def ring(block, axis, halves, ready=lambda *v: v):
    after, before = ready(shift(block, axis, -1), shift(block, axis, 1))
    return block, after, before, shift(halves(before)[0], axis, 1), shift(halves(after)[1], axis, -1)


def moments(piece):
    value = piece.astype(jnp.float32)
    mean = jnp.mean(value, axis=-1)
    return mean, jnp.sum((value - mean[..., None]) ** 2, axis=-1)


def merge(stats, count):
    means = [s[0] for s in stats]
    centre = 0.25 * (means[0] + means[1] + means[2] + means[3])
    total = stats[0][1] + stats[1][1] + stats[2][1] + stats[3][1]
    for m in means:
        total = total + count * (m - centre) ** 2
    return centre, total


def shards(tokens, ln_gain, w_qkv, q_gain, k_gain, w_up, w_out, w_down):
    y, x, h, l, c = (lax.axis_index(a) for a in ("y", "x", "h", "l", "c"))
    slot = jnp.where(l == h, 1, 0)
    index = jnp.stack([y, slot, c, x, (y - x + 4) % 4, l]).astype(jnp.int32)

    up_all = lax.all_gather(w_up[None], "y", axis=0)
    qkv_all = lax.all_gather(w_qkv.transpose(1, 0, 2), "y", axis=0)

    block_a = move_z(tokens, [(1, 0), (0, 2), (3, 1), (2, 3)])
    block_b = move_z(tokens, [(0, 0), (1, 2), (2, 1), (3, 3)])
    out_pieces = [w_out] + [shift(w_out, "y", -o) for o in STEPS[1:]]
    held = after(jnp.stack([block_a, block_b]), *out_pieces)
    own = ring(held, "x", lambda v: (v[0], v[1]))
    other = [shift(piece, "c", 1) for piece in own]

    parts = [moments(piece) for piece in own]
    last = [jnp.stack([a, b]) for a, b in zip(parts[3], parts[4])]
    stats = jnp.stack(merge([*parts[:3], last], 384))
    cross = lax.ppermute(stats, ("l", "c"), [(i, 3 - i) for i in range(4)])
    centre, spread = merge([stats, shift(stats, "c", 1), shift(stats, "l", 1), cross], 1536)
    centre, scale = lax.optimization_barrier((centre, lax.rsqrt(spread / 6144 + EPS)))
    gain = ln_gain.reshape(4, 2, 2, 1, 384)

    up_sum, up_sent, features = project(
        index, own, other, centre[..., None], scale[..., None], gain, up_all
    )
    pre_act = up_sum + shift(up_sent, "l", 1).astype(jnp.float32)
    activated = jax.nn.gelu(pre_act, approximate=False).astype(jnp.bfloat16)

    qkv_mine, qkv_theirs = project_again(index, features, qkv_all)

    w_down = after(w_down, qkv_all)
    after_w, before_w = after((shift(w_down, "y", -1), shift(w_down, "y", 1)), activated)
    forward = before_w[:384], after_w[384:]
    down = w_down, after_w, before_w, shift(forward[0], "y", 1), shift(forward[1], "y", -1)

    got = after(shift(qkv_theirs, "l", 1), activated, *forward)
    attended = attend(qkv_mine, got, q_gain, k_gain)
    attended_other = shift(attended, "l", 1)

    def start_terms(block):
        keep, send = output_terms(
            index, block, attended, attended_other, activated, out_pieces, down
        )
        return keep, shift(send, "c", 1)

    def start_sums(keep, got):
        pair = [keep[o].astype(jnp.float32) + got[o].astype(jnp.float32) for o in range(4)]
        far = pair[2].astype(jnp.bfloat16)
        return pair, shift(far[:256], "x", 1), shift(far[256:], "x", -1)

    def finish_sums(pair, first, second, pairs):
        f32 = lambda v: v.astype(jnp.float32)
        up = jnp.concatenate([pair[1][:256] + f32(first), pair[1][256:]]).astype(jnp.bfloat16)
        down = jnp.concatenate([pair[3][:256], pair[3][256:] + f32(second)]).astype(jnp.bfloat16)
        summed = pair[0] + f32(shift(up, "x", 1)) + f32(shift(down, "x", -1))
        return f32(move_z(summed.astype(jnp.bfloat16), pairs))

    keep_a, got_a = start_terms(0)
    keep_b, got_b = start_terms(1)
    sums_a = start_sums(keep_a, got_a)
    sums_b = start_sums(keep_b, got_b)
    part_a = finish_sums(*sums_a, [(0, 1), (2, 0), (1, 3), (3, 2)])
    part_b = finish_sums(*sums_b, [(0, 0), (2, 1), (1, 2), (3, 3)])
    return (tokens.astype(jnp.float32) + part_a + part_b).astype(jnp.bfloat16)


def solution(mesh):
    fine = Mesh(mesh.devices.reshape(4, 2, 4, 2, 2), AXES)
    row, col = ("y", "l"), ("x", "h", "c")
    in_specs = (
        P(row, col),
        P(),
        P(row, None, col),
        P(),
        P(),
        P(row, col),
        P(col, row),
        P(col, row),
    )
    return jax.shard_map(shards, mesh=fine, in_specs=in_specs, out_specs=P(row, col), check_vma=False)
```

```python
import functools
import math

import jax
import jax.numpy as jnp
from jax import lax
from jax.experimental import pallas as pl
from jax.experimental.pallas import tpu as pltpu
from jax.sharding import Mesh, PartitionSpec as P

HD = 128
PATCHES = 256
EPS = 1e-06
AXES = ("y", "l", "x", "h", "c")
SIZES = {"y": 4, "l": 2, "x": 4, "h": 2, "c": 2}
VMEM_LIMIT = 56 << 20
STEPS = (0, 1, 3, 2)
ROWS = 768


def shift(value, axis, by):
    size = SIZES[axis]
    return lax.ppermute(value, axis, [(i, (i + by) % size) for i in range(size)])


def move_z(value, pairs):
    place = lambda z: (z & 1) * 2 + (z >> 1)
    return lax.ppermute(value, ("l", "h"), [(place(s), place(d)) for s, d in pairs])


def norm_rows(value, gain):
    centre = jnp.mean(value, axis=-1, keepdims=True)
    deviation = value - centre
    variance = jnp.mean(deviation * deviation, axis=-1, keepdims=True)
    return deviation * lax.rsqrt(variance + EPS) * gain


def project_kernel(index, *refs):
    own, other, (stats, gain, w_ref) = refs[0:5], refs[5:10], refs[10:13]
    sum_ref, sent_ref, block_ref, turned = refs[13:]
    step, core = pl.program_id(0), index[2]

    @pl.when(step == 0)
    def _():
        turned[...] = stats[...].T

    for j in range(4):

        @pl.when(step == j)
        def _():
            for pieces, place in ((own, core), (other, 1 - core)):
                for t in range(2):
                    raw = pieces[3 + t][...] if j == 3 else pieces[j][t]
                    centre, scale = turned[:, t : t + 1], turned[:, 2 + t : 3 + t]
                    value = (raw.astype(jnp.float32) - centre) * scale * gain[0, 0, place]
                    block_ref[0, place, t * 512 : (t + 1) * 512] = value.astype(jnp.bfloat16)

    multiply(step, block_ref, w_ref, sum_ref)

    @pl.when(step == 3)
    def _():
        sent_ref[...] = sum_ref[...].astype(jnp.bfloat16)


def project_again_kernel(index, block_ref, w_ref, mine_ref, theirs_ref, acc_ref):
    step = pl.program_id(0)
    multiply(step, block_ref, w_ref, acc_ref)
    finish(step, index, acc_ref, mine_ref, theirs_ref)


def multiply(step, block_ref, w_ref, acc_ref):
    groups, width = w_ref.shape[1], w_ref.shape[-1]

    @pl.when(step == 0)
    def _():
        acc_ref[...] = jnp.zeros_like(acc_ref)

    for g in range(groups):
        cols = slice(g * width, (g + 1) * width)
        part = jnp.dot(block_ref[0, 0], w_ref[0, g, :384], preferred_element_type=jnp.float32)
        part += jnp.dot(block_ref[0, 1], w_ref[0, g, 384:], preferred_element_type=jnp.float32)
        acc_ref[:, :, cols] += part.reshape(2, 512, width)


def finish(step, index, acc_ref, mine_ref, theirs_ref):
    @pl.when(step == 3)
    def _():
        slot = index[1]
        mine_ref[...] = acc_ref[slot]
        theirs_ref[...] = acc_ref[1 - slot].astype(jnp.bfloat16)


def call(kernel, index, arrays, specs, outs, out_specs, scratch, flops):
    size = lambda a: math.prod(a.shape) * a.dtype.itemsize
    whole = lambda a: pl.BlockSpec(a.shape, lambda j, i, n=len(a.shape): (0,) * n)
    return pl.pallas_call(
        kernel,
        out_shape=outs,
        grid_spec=pltpu.PrefetchScalarGridSpec(
            num_scalar_prefetch=1,
            grid=(4,),
            in_specs=[spec or whole(a) for a, spec in zip(arrays, specs)],
            out_specs=[spec or whole(a) for a, spec in zip(outs, out_specs)],
            scratch_shapes=scratch,
        ),
        compiler_params=pltpu.CompilerParams(vmem_limit_bytes=VMEM_LIMIT),
        cost_estimate=pl.CostEstimate(
            flops=flops,
            bytes_accessed=sum(map(size, arrays)) + sum(map(size, outs)),
            transcendentals=0,
        ),
    )(index, *arrays)


def order(j):
    return j + (j == 2) * 1 - (j == 3) * 1


def by_block(which, *shape):
    return pl.BlockSpec((1, *shape), lambda j, i: ((i[which] + order(j)) % 4,) + (0,) * len(shape))


PARTS = [jax.ShapeDtypeStruct((512, ROWS), t) for t in (jnp.float32, jnp.bfloat16)]
SUMS = [pltpu.VMEM((2, 512, ROWS), jnp.float32)]
BY_STEP = pl.BlockSpec((1, 2, 1024, 384), lambda j, i: (j, 0, 0, 0))


def project(index, own, other, stats, gain, weights):
    return call(
        project_kernel,
        index,
        [*own, *other, stats, gain, weights],
        [None] * 11
        + [pl.BlockSpec((1, 1, 2, 1, 384), lambda j, i: ((i[3] + order(j)) % 4, i[5], 0, 0, 0))]
        + [by_block(3, *weights.shape[1:])],
        [
            jax.ShapeDtypeStruct((2, 512, ROWS), jnp.float32),
            jax.ShapeDtypeStruct((2, 512, ROWS), jnp.bfloat16),
            jax.ShapeDtypeStruct((4, 2, 1024, 384), jnp.bfloat16),
        ],
        [None, None, BY_STEP],
        [pltpu.VMEM((512, 8), jnp.float32)],
        2 * 1024 * 3072 * ROWS,
    )


def project_again(index, features, weights):
    return call(
        project_again_kernel,
        index,
        [features, weights],
        [BY_STEP, by_block(3, *weights.shape[1:])],
        PARTS,
        [None, None],
        SUMS,
        2 * 1024 * 3072 * ROWS,
    )


def attend_kernel(mine_ref, got_ref, q_gain_ref, k_gain_ref, out_ref):
    for frame in range(2):
        rows = slice(frame * PATCHES, (frame + 1) * PATCHES)
        for head in range(2):

            def part(which):
                cols = slice(which * 256 + head * HD, which * 256 + (head + 1) * HD)
                return mine_ref[rows, cols] + got_ref[rows, cols].astype(jnp.float32)

            queries = norm_rows(part(0), q_gain_ref[...]).astype(jnp.bfloat16)
            key_vecs = norm_rows(part(1), k_gain_ref[...]).astype(jnp.bfloat16)
            scores = lax.dot_general(
                queries, key_vecs, (((1,), (1,)), ((), ())), preferred_element_type=jnp.float32
            ) / math.sqrt(HD)
            exponent = jnp.exp(scores)
            probs = (exponent / jnp.sum(exponent, axis=-1, keepdims=True)).astype(jnp.bfloat16)
            out_ref[rows, head * HD : (head + 1) * HD] = jnp.dot(
                probs, part(2).astype(jnp.bfloat16), preferred_element_type=jnp.float32
            ).astype(jnp.bfloat16)


def attend(mine, got, q_gain, k_gain):
    return pl.pallas_call(
        attend_kernel,
        out_shape=jax.ShapeDtypeStruct((512, 256), jnp.bfloat16),
        compiler_params=pltpu.CompilerParams(vmem_limit_bytes=VMEM_LIMIT),
        cost_estimate=pl.CostEstimate(
            flops=4 * 4 * 256 * 256 * 128, bytes_accessed=512 * 768 * 6, transcendentals=4 * 256 * 256
        ),
    )(mine, got, q_gain.reshape(1, HD), k_gain.reshape(1, HD))


def output_kernel(index, att_own, att_other, act_ref, w_down, *refs):
    w_out, w_rest, outs, w_ref = refs[:5], refs[5:9], refs[9:13], refs[13]
    step, first = pl.program_id(0), index[2] == 0
    for j in range(4):

        @pl.when(step == j)
        def _():
            if j == 3:
                w_ref[:128] = w_out[3][...]
                w_ref[128:256] = w_out[4][...]
            else:
                w_ref[:256] = w_out[j][...]
            w_ref[256:] = w_rest[j][...]

    for block in range(2):
        att = jnp.where(index[1] == block, att_own[...], att_other[...])
        term = jnp.dot(act_ref[block, :, :512], w_down[0], preferred_element_type=jnp.float32)
        mixed = jnp.concatenate([att, act_ref[block, :, 512:]], axis=1)
        term += jnp.dot(mixed, w_ref[...], preferred_element_type=jnp.float32)
        term = term.astype(jnp.bfloat16)
        outs[2 * block][0] = jnp.where(first, term[:, :384], term[:, 384:])
        outs[2 * block + 1][0] = jnp.where(first, term[:, 384:], term[:, :384])


def output_terms(index, att_own, att_other, activated, w_down, w_out, w_rest):
    out = jax.ShapeDtypeStruct((4, 512, 384), jnp.bfloat16)
    out_spec = pl.BlockSpec((1, 512, 384), lambda j, i: ((i[4] + order(j)) % 4, 0, 0))
    return call(
        output_kernel,
        index,
        [att_own, att_other, activated, w_down, *w_out, *w_rest],
        [None] * 3 + [by_block(0, 512, ROWS)] + [None] * 9,
        [out] * 4,
        [out_spec] * 4,
        [pltpu.VMEM((512, ROWS), jnp.bfloat16)],
        2 * 1024 * 1024 * 4 * ROWS,
    )


def after(value, *others):
    return lax.optimization_barrier((value, *others))[0]


def ring(block, axis, halves, ready=lambda *v: v):
    after, before = ready(shift(block, axis, -1), shift(block, axis, 1))
    return block, after, before, shift(halves(before)[0], axis, 1), shift(halves(after)[1], axis, -1)


def moments(piece):
    value = piece.astype(jnp.float32)
    mean = jnp.mean(value, axis=-1)
    return mean, jnp.sum((value - mean[..., None]) ** 2, axis=-1)


def merge(stats, count):
    means = [s[0] for s in stats]
    centre = 0.25 * (means[0] + means[1] + means[2] + means[3])
    total = stats[0][1] + stats[1][1] + stats[2][1] + stats[3][1]
    for m in means:
        total = total + count * (m - centre) ** 2
    return centre, total


def shards(tokens, ln_gain, w_qkv, q_gain, k_gain, w_up, w_out, w_down):
    y, x, h, l, c = (lax.axis_index(a) for a in ("y", "x", "h", "l", "c"))
    slot = jnp.where(l == h, 1, 0)
    index = jnp.stack([y, slot, c, x, (y - x + 4) % 4, l]).astype(jnp.int32)

    up_all = lax.all_gather(w_up[None], "y", axis=0)
    qkv_all = lax.all_gather(w_qkv.transpose(1, 0, 2), "y", axis=0)
    down_all = lax.all_gather(w_down[:512], "y", axis=0)

    block_a = move_z(tokens, [(1, 0), (0, 2), (3, 1), (2, 3)])
    block_b = move_z(tokens, [(0, 0), (1, 2), (2, 1), (3, 3)])
    out_near = shift(w_out, "y", -1), shift(w_out, "y", 1)
    own = ring(after(jnp.stack([block_a, block_b]), *out_near), "x", lambda v: (v[0], v[1]))
    other = [shift(piece, "c", 1) for piece in own]

    parts = [moments(piece) for piece in own]
    last = [jnp.stack([a, b]) for a, b in zip(parts[3], parts[4])]
    stats = jnp.stack(merge([*parts[:3], last], 384))
    cross = lax.ppermute(stats, ("l", "c"), [(i, 3 - i) for i in range(4)])
    centre, spread = merge([stats, shift(stats, "c", 1), shift(stats, "l", 1), cross], 1536)
    stats = jnp.concatenate([centre, lax.rsqrt(spread / 6144 + EPS), centre, centre])
    gain = ln_gain.reshape(4, 2, 2, 1, 384)

    up_sum, up_sent, features = project(
        index, own, other, stats, gain, up_all
    )
    out_near = after(out_near, up_sum)
    out_far = shift(out_near[1][:128], "y", 1), shift(out_near[0][128:], "y", -1)
    out_pieces = w_out, *out_near, *out_far
    qkv_all = after(qkv_all, *out_far)
    rest = after(w_down[512:], qkv_all)
    down_pieces = [rest] + [shift(rest, "y", -o) for o in STEPS[1:]]

    pre_act = up_sum + shift(up_sent, "l", 1).astype(jnp.float32)
    activated = jax.nn.gelu(pre_act, approximate=False).astype(jnp.bfloat16)

    qkv_mine, qkv_theirs = project_again(index, features, qkv_all)
    got = after(shift(qkv_theirs, "l", 1), activated)
    attended = attend(qkv_mine, got, q_gain, k_gain)
    attended_other = shift(attended, "l", 1)

    def start_sums(keep, got):
        pair = [keep[o].astype(jnp.float32) + got[o].astype(jnp.float32) for o in range(4)]
        far = pair[2].astype(jnp.bfloat16)
        return pair, shift(far[:256], "x", 1), shift(far[256:], "x", -1)

    def finish_sums(pair, first, second, pairs):
        f32 = lambda v: v.astype(jnp.float32)
        up = jnp.concatenate([pair[1][:256] + f32(first), pair[1][256:]]).astype(jnp.bfloat16)
        down = jnp.concatenate([pair[3][:256], pair[3][256:] + f32(second)]).astype(jnp.bfloat16)
        summed = pair[0] + f32(shift(up, "x", 1)) + f32(shift(down, "x", -1))
        return f32(move_z(summed.astype(jnp.bfloat16), pairs))

    keep_a, send_a, keep_b, send_b = output_terms(
        index, attended, attended_other, activated, down_all, out_pieces, down_pieces
    )
    sums_a = start_sums(keep_a, shift(send_a, "c", 1))
    sums_b = start_sums(keep_b, shift(send_b, "c", 1))
    part_a = finish_sums(*sums_a, [(0, 1), (2, 0), (1, 3), (3, 2)])
    part_b = finish_sums(*sums_b, [(0, 0), (2, 1), (1, 2), (3, 3)])
    return (tokens.astype(jnp.float32) + part_a + part_b).astype(jnp.bfloat16)


def solution(mesh):
    fine = Mesh(mesh.devices.reshape(4, 2, 4, 2, 2), AXES)
    row, col = ("y", "l"), ("x", "h", "c")
    in_specs = (
        P(row, col),
        P(),
        P(row, None, col),
        P(),
        P(),
        P(row, col),
        P(col, row),
        P(col, row),
    )
    return jax.shard_map(shards, mesh=fine, in_specs=in_specs, out_specs=P(row, col), check_vma=False)
```

```python
import functools
import math

import jax
import jax.numpy as jnp
from jax import lax
from jax.experimental import pallas as pl
from jax.experimental.pallas import tpu as pltpu
from jax.sharding import Mesh, PartitionSpec as P

HD = 128
PATCHES = 256
EPS = 1e-06
AXES = ("y", "l", "x", "h", "c")
SIZES = {"y": 4, "l": 2, "x": 4, "h": 2, "c": 2}
VMEM_LIMIT = 56 << 20
STEPS = (0, 1, 3, 2)
ROWS = 768


def shift(value, axis, by):
    size = SIZES[axis]
    return lax.ppermute(value, axis, [(i, (i + by) % size) for i in range(size)])


def move_z(value, pairs):
    place = lambda z: (z & 1) * 2 + (z >> 1)
    return lax.ppermute(value, ("l", "h"), [(place(s), place(d)) for s, d in pairs])


def norm_rows(value, gain):
    centre = jnp.mean(value, axis=-1, keepdims=True)
    deviation = value - centre
    variance = jnp.mean(deviation * deviation, axis=-1, keepdims=True)
    return deviation * lax.rsqrt(variance + EPS) * gain


def project_kernel(index, *refs):
    own, other, (stats, gain, w_ref) = refs[0:5], refs[5:10], refs[10:13]
    sum_ref, sent_ref, block_ref, turned = refs[13:]
    step, core = pl.program_id(0), index[2]

    @pl.when(step == 0)
    def _():
        turned[...] = stats[...].T

    for j in range(4):

        @pl.when(step == j)
        def _():
            for pieces, place in ((own, core), (other, 1 - core)):
                for t in range(2):
                    raw = pieces[3 + t][...] if j == 3 else pieces[j][t]
                    centre, scale = turned[:, t : t + 1], turned[:, 2 + t : 3 + t]
                    value = (raw.astype(jnp.float32) - centre) * scale * gain[0, 0, place]
                    block_ref[0, place, t * 512 : (t + 1) * 512] = value.astype(jnp.bfloat16)

    multiply(step, block_ref, w_ref, sum_ref)

    @pl.when(step == 3)
    def _():
        sent_ref[...] = sum_ref[...].astype(jnp.bfloat16)


def project_again_kernel(index, block_ref, w_ref, mine_ref, theirs_ref, acc_ref):
    step = pl.program_id(0)
    multiply(step, block_ref, w_ref, acc_ref)
    finish(step, index, acc_ref, mine_ref, theirs_ref)


def multiply(step, block_ref, w_ref, acc_ref):
    groups, width = w_ref.shape[1], w_ref.shape[-1]

    @pl.when(step == 0)
    def _():
        acc_ref[...] = jnp.zeros_like(acc_ref)

    for g in range(groups):
        cols = slice(g * width, (g + 1) * width)
        part = jnp.dot(block_ref[0, 0], w_ref[0, g, :384], preferred_element_type=jnp.float32)
        part += jnp.dot(block_ref[0, 1], w_ref[0, g, 384:], preferred_element_type=jnp.float32)
        acc_ref[:, :, cols] += part.reshape(2, 512, width)


def finish(step, index, acc_ref, mine_ref, theirs_ref):
    @pl.when(step == 3)
    def _():
        slot = index[1]
        mine_ref[...] = acc_ref[slot]
        theirs_ref[...] = acc_ref[1 - slot].astype(jnp.bfloat16)


def call(kernel, index, arrays, specs, outs, out_specs, scratch, flops, vmem=VMEM_LIMIT):
    size = lambda a: math.prod(a.shape) * a.dtype.itemsize
    whole = lambda a: pl.BlockSpec(a.shape, lambda j, i, n=len(a.shape): (0,) * n)
    return pl.pallas_call(
        kernel,
        out_shape=outs,
        grid_spec=pltpu.PrefetchScalarGridSpec(
            num_scalar_prefetch=1,
            grid=(4,),
            in_specs=[spec or whole(a) for a, spec in zip(arrays, specs)],
            out_specs=[spec or whole(a) for a, spec in zip(outs, out_specs)],
            scratch_shapes=scratch,
        ),
        compiler_params=pltpu.CompilerParams(vmem_limit_bytes=vmem),
        cost_estimate=pl.CostEstimate(
            flops=flops,
            bytes_accessed=sum(map(size, arrays)) + sum(map(size, outs)),
            transcendentals=0,
        ),
    )(index, *arrays)


def order(j):
    return j + (j == 2) * 1 - (j == 3) * 1


def by_block(which, *shape):
    return pl.BlockSpec((1, *shape), lambda j, i: ((i[which] + order(j)) % 4,) + (0,) * len(shape))


PARTS = [jax.ShapeDtypeStruct((512, ROWS), t) for t in (jnp.float32, jnp.bfloat16)]
SUMS = [pltpu.VMEM((2, 512, ROWS), jnp.float32)]
BY_STEP = pl.BlockSpec((1, 2, 1024, 384), lambda j, i: (j, 0, 0, 0))


def project(index, own, other, stats, gain, weights):
    return call(
        project_kernel,
        index,
        [*own, *other, stats, gain, weights],
        [None] * 11
        + [pl.BlockSpec((1, 1, 2, 1, 384), lambda j, i: ((i[3] + order(j)) % 4, i[5], 0, 0, 0))]
        + [by_block(3, *weights.shape[1:])],
        [
            jax.ShapeDtypeStruct((2, 512, ROWS), jnp.float32),
            jax.ShapeDtypeStruct((2, 512, ROWS), jnp.bfloat16),
            jax.ShapeDtypeStruct((4, 2, 1024, 384), jnp.bfloat16),
        ],
        [None, None, BY_STEP],
        [pltpu.VMEM((512, 8), jnp.float32)],
        2 * 1024 * 3072 * ROWS,
    )


def project_again(index, features, weights):
    return call(
        project_again_kernel,
        index,
        [features, weights],
        [BY_STEP, by_block(3, *weights.shape[1:])],
        PARTS,
        [None, None],
        SUMS,
        2 * 1024 * 3072 * ROWS,
    )


def attend_kernel(mine_ref, got_ref, q_gain_ref, k_gain_ref, out_ref):
    for frame in range(2):
        rows = slice(frame * PATCHES, (frame + 1) * PATCHES)
        for head in range(2):

            def part(which):
                cols = slice(which * 256 + head * HD, which * 256 + (head + 1) * HD)
                return mine_ref[rows, cols] + got_ref[rows, cols].astype(jnp.float32)

            queries = norm_rows(part(0), q_gain_ref[...]).astype(jnp.bfloat16)
            key_vecs = norm_rows(part(1), k_gain_ref[...]).astype(jnp.bfloat16)
            scores = lax.dot_general(
                queries, key_vecs, (((1,), (1,)), ((), ())), preferred_element_type=jnp.float32
            ) / math.sqrt(HD)
            exponent = jnp.exp(scores)
            probs = (exponent / jnp.sum(exponent, axis=-1, keepdims=True)).astype(jnp.bfloat16)
            out_ref[rows, head * HD : (head + 1) * HD] = jnp.dot(
                probs, part(2).astype(jnp.bfloat16), preferred_element_type=jnp.float32
            ).astype(jnp.bfloat16)


def attend(mine, got, q_gain, k_gain):
    return pl.pallas_call(
        attend_kernel,
        out_shape=jax.ShapeDtypeStruct((512, 256), jnp.bfloat16),
        compiler_params=pltpu.CompilerParams(vmem_limit_bytes=VMEM_LIMIT),
        cost_estimate=pl.CostEstimate(
            flops=4 * 4 * 256 * 256 * 128, bytes_accessed=512 * 768 * 6, transcendentals=4 * 256 * 256
        ),
    )(mine, got, q_gain.reshape(1, HD), k_gain.reshape(1, HD))


def output_kernel(index, att_own, att_other, act_ref, w_down, *refs):
    w_out, w_rest, outs, w_ref = refs[:5], refs[5:9], refs[9:13], refs[13]
    step, first = pl.program_id(0), index[2] == 0
    for j in range(4):

        @pl.when(step == j)
        def _():
            if j == 3:
                w_ref[:128] = w_out[3][...]
                w_ref[128:256] = w_out[4][...]
            else:
                w_ref[:256] = w_out[j][...]
            w_ref[256:] = w_rest[j][...]

    own_first = index[1] == 0
    att = jnp.concatenate(
        [
            jnp.where(own_first, att_own[...], att_other[...]),
            jnp.where(own_first, att_other[...], att_own[...]),
        ]
    )
    act = act_ref[...].reshape(1024, ROWS)
    term = jnp.dot(act[:, :512], w_down[0], preferred_element_type=jnp.float32)
    mixed = jnp.concatenate([att, act[:, 512:]], axis=1)
    term += jnp.dot(mixed, w_ref[...], preferred_element_type=jnp.float32)
    term = term.astype(jnp.bfloat16)
    for block in range(2):
        part = term[block * 512 : (block + 1) * 512]
        outs[2 * block][0] = jnp.where(first, part[:, :384], part[:, 384:])
        outs[2 * block + 1][0] = jnp.where(first, part[:, 384:], part[:, :384])


def output_terms(index, att_own, att_other, activated, w_down, w_out, w_rest):
    out = jax.ShapeDtypeStruct((4, 512, 384), jnp.bfloat16)
    out_spec = pl.BlockSpec((1, 512, 384), lambda j, i: ((i[4] + order(j)) % 4, 0, 0))
    return call(
        output_kernel,
        index,
        [att_own, att_other, activated, w_down, *w_out, *w_rest],
        [None] * 3 + [by_block(0, 512, ROWS)] + [None] * 9,
        [out] * 4,
        [out_spec] * 4,
        [pltpu.VMEM((512, ROWS), jnp.bfloat16)],
        2 * 1024 * 1024 * 4 * ROWS,
        vmem=50 << 20,
    )


def after(value, *others):
    return lax.optimization_barrier((value, *others))[0]


def ring(block, axis, halves, ready=lambda *v: v):
    after, before = ready(shift(block, axis, -1), shift(block, axis, 1))
    return block, after, before, shift(halves(before)[0], axis, 1), shift(halves(after)[1], axis, -1)


def moments(piece):
    value = piece.astype(jnp.float32)
    mean = jnp.mean(value, axis=-1)
    return mean, jnp.sum((value - mean[..., None]) ** 2, axis=-1)


def merge(stats, count):
    means = [s[0] for s in stats]
    centre = 0.25 * (means[0] + means[1] + means[2] + means[3])
    total = stats[0][1] + stats[1][1] + stats[2][1] + stats[3][1]
    for m in means:
        total = total + count * (m - centre) ** 2
    return centre, total


def shards(tokens, ln_gain, w_qkv, q_gain, k_gain, w_up, w_out, w_down):
    y, x, h, l, c = (lax.axis_index(a) for a in ("y", "x", "h", "l", "c"))
    slot = jnp.where(l == h, 1, 0)
    index = jnp.stack([y, slot, c, x, (y - x + 4) % 4, l]).astype(jnp.int32)

    up_all = lax.all_gather(w_up[None], "y", axis=0)
    qkv_all = lax.all_gather(w_qkv.transpose(1, 0, 2), "y", axis=0)
    down_all = lax.all_gather(w_down[:512], "y", axis=0)

    block_a = move_z(tokens, [(1, 0), (0, 2), (3, 1), (2, 3)])
    block_b = move_z(tokens, [(0, 0), (1, 2), (2, 1), (3, 3)])
    out_near = shift(w_out, "y", -1), shift(w_out, "y", 1)
    own = ring(after(jnp.stack([block_a, block_b]), *out_near), "x", lambda v: (v[0], v[1]))
    other = [shift(piece, "c", 1) for piece in own]

    parts = [moments(piece) for piece in own]
    last = [jnp.stack([a, b]) for a, b in zip(parts[3], parts[4])]
    stats = jnp.stack(merge([*parts[:3], last], 384))
    cross = lax.ppermute(stats, ("l", "c"), [(i, 3 - i) for i in range(4)])
    centre, spread = merge([stats, shift(stats, "c", 1), shift(stats, "l", 1), cross], 1536)
    stats = jnp.concatenate([centre, lax.rsqrt(spread / 6144 + EPS), centre, centre])
    gain = ln_gain.reshape(4, 2, 2, 1, 384)

    up_sum, up_sent, features = project(
        index, own, other, stats, gain, up_all
    )
    out_near = after(out_near, up_sum)
    out_far = shift(out_near[1][:128], "y", 1), shift(out_near[0][128:], "y", -1)
    out_pieces = w_out, *out_near, *out_far
    qkv_all = after(qkv_all, *out_far)
    rest = after(w_down[512:], qkv_all)
    down_pieces = [rest] + [shift(rest, "y", -o) for o in STEPS[1:]]

    pre_act = up_sum + shift(up_sent, "l", 1).astype(jnp.float32)
    activated = jax.nn.gelu(pre_act, approximate=False).astype(jnp.bfloat16)

    qkv_mine, qkv_theirs = project_again(index, features, qkv_all)
    got = after(shift(qkv_theirs, "l", 1), activated)
    attended = attend(qkv_mine, got, q_gain, k_gain)
    attended_other = shift(attended, "l", 1)

    def start_sums(keep, got):
        pair = [keep[o].astype(jnp.float32) + got[o].astype(jnp.float32) for o in range(4)]
        far = pair[2].astype(jnp.bfloat16)
        return pair, shift(far[:256], "x", 1), shift(far[256:], "x", -1)

    def finish_sums(pair, first, second, pairs):
        f32 = lambda v: v.astype(jnp.float32)
        up = jnp.concatenate([pair[1][:256] + f32(first), pair[1][256:]]).astype(jnp.bfloat16)
        down = jnp.concatenate([pair[3][:256], pair[3][256:] + f32(second)]).astype(jnp.bfloat16)
        summed = pair[0] + f32(shift(up, "x", 1)) + f32(shift(down, "x", -1))
        return f32(move_z(summed.astype(jnp.bfloat16), pairs))

    keep_a, send_a, keep_b, send_b = output_terms(
        index, attended, attended_other, activated, down_all, out_pieces, down_pieces
    )
    sums_a = start_sums(keep_a, shift(send_a, "c", 1))
    sums_b = start_sums(keep_b, shift(send_b, "c", 1))
    part_a = finish_sums(*sums_a, [(0, 1), (2, 0), (1, 3), (3, 2)])
    part_b = finish_sums(*sums_b, [(0, 0), (2, 1), (1, 2), (3, 3)])
    return (tokens.astype(jnp.float32) + part_a + part_b).astype(jnp.bfloat16)


def solution(mesh):
    fine = Mesh(mesh.devices.reshape(4, 2, 4, 2, 2), AXES)
    row, col = ("y", "l"), ("x", "h", "c")
    in_specs = (
        P(row, col),
        P(),
        P(row, None, col),
        P(),
        P(),
        P(row, col),
        P(col, row),
        P(col, row),
    )
    return jax.shard_map(shards, mesh=fine, in_specs=in_specs, out_specs=P(row, col), check_vma=False)
```

```python
import functools
import math

import jax
import jax.numpy as jnp
from jax import lax
from jax.experimental import pallas as pl
from jax.experimental.pallas import tpu as pltpu
from jax.sharding import Mesh, PartitionSpec as P

HD = 128
PATCHES = 256
EPS = 1e-06
AXES = ("y", "l", "x", "h", "c")
SIZES = {"y": 4, "l": 2, "x": 4, "h": 2, "c": 2}
VMEM_LIMIT = 56 << 20
STEPS = (0, 1, 3, 2)
ROWS = 768


def shift(value, axis, by):
    size = SIZES[axis]
    return lax.ppermute(value, axis, [(i, (i + by) % size) for i in range(size)])


def move_z(value, pairs):
    place = lambda z: (z & 1) * 2 + (z >> 1)
    return lax.ppermute(value, ("l", "h"), [(place(s), place(d)) for s, d in pairs])


def norm_rows(value, gain):
    centre = jnp.mean(value, axis=-1, keepdims=True)
    deviation = value - centre
    variance = jnp.mean(deviation * deviation, axis=-1, keepdims=True)
    return deviation * lax.rsqrt(variance + EPS) * gain


def project_kernel(index, *refs):
    own, other, (stats, gain, w_ref) = refs[0:5], refs[5:10], refs[10:13]
    sum_ref, sent_ref, block_ref, turned = refs[13:]
    step, core = pl.program_id(0), index[2]

    @pl.when(step == 0)
    def _():
        turned[...] = stats[...].T

    for j in range(4):

        @pl.when(step == j)
        def _():
            for pieces, place in ((own, core), (other, 1 - core)):
                for t in range(2):
                    raw = pieces[3 + t][...] if j == 3 else pieces[j][t]
                    centre, scale = turned[:, t : t + 1], turned[:, 2 + t : 3 + t]
                    value = (raw.astype(jnp.float32) - centre) * scale * gain[0, 0, place]
                    block_ref[0, place, t * 512 : (t + 1) * 512] = value.astype(jnp.bfloat16)

    multiply(step, block_ref, w_ref, sum_ref)

    @pl.when(step == 3)
    def _():
        sent_ref[...] = sum_ref[...].astype(jnp.bfloat16)


def project_again_kernel(index, block_ref, w_ref, mine_ref, theirs_ref, acc_ref):
    step = pl.program_id(0)
    multiply(step, block_ref, w_ref, acc_ref)
    finish(step, index, acc_ref, mine_ref, theirs_ref)


def multiply(step, block_ref, w_ref, acc_ref):
    groups, width = w_ref.shape[1], w_ref.shape[-1]

    @pl.when(step == 0)
    def _():
        acc_ref[...] = jnp.zeros_like(acc_ref)

    for g in range(groups):
        cols = slice(g * width, (g + 1) * width)
        part = jnp.dot(block_ref[0, 0], w_ref[0, g, :384], preferred_element_type=jnp.float32)
        part += jnp.dot(block_ref[0, 1], w_ref[0, g, 384:], preferred_element_type=jnp.float32)
        acc_ref[:, :, cols] += part.reshape(2, 512, width)


def finish(step, index, acc_ref, mine_ref, theirs_ref):
    @pl.when(step == 3)
    def _():
        slot = index[1]
        mine_ref[...] = acc_ref[slot]
        theirs_ref[...] = acc_ref[1 - slot].astype(jnp.bfloat16)


def call(kernel, index, arrays, specs, outs, out_specs, scratch, flops, vmem=VMEM_LIMIT):
    size = lambda a: math.prod(a.shape) * a.dtype.itemsize
    whole = lambda a: pl.BlockSpec(a.shape, lambda j, i, n=len(a.shape): (0,) * n)
    return pl.pallas_call(
        kernel,
        out_shape=outs,
        grid_spec=pltpu.PrefetchScalarGridSpec(
            num_scalar_prefetch=1,
            grid=(4,),
            in_specs=[spec or whole(a) for a, spec in zip(arrays, specs)],
            out_specs=[spec or whole(a) for a, spec in zip(outs, out_specs)],
            scratch_shapes=scratch,
        ),
        compiler_params=pltpu.CompilerParams(vmem_limit_bytes=vmem),
        cost_estimate=pl.CostEstimate(
            flops=flops,
            bytes_accessed=sum(map(size, arrays)) + sum(map(size, outs)),
            transcendentals=0,
        ),
    )(index, *arrays)


def order(j):
    return j + (j == 2) * 1 - (j == 3) * 1


def by_block(which, *shape):
    return pl.BlockSpec((1, *shape), lambda j, i: ((i[which] + order(j)) % 4,) + (0,) * len(shape))


PARTS = [jax.ShapeDtypeStruct((512, ROWS), t) for t in (jnp.float32, jnp.bfloat16)]
SUMS = [pltpu.VMEM((2, 512, ROWS), jnp.float32)]
BY_STEP = pl.BlockSpec((1, 2, 1024, 384), lambda j, i: (j, 0, 0, 0))


def project(index, own, other, stats, gain, weights):
    return call(
        project_kernel,
        index,
        [*own, *other, stats, gain, weights],
        [None] * 11
        + [pl.BlockSpec((1, 1, 2, 1, 384), lambda j, i: ((i[3] + order(j)) % 4, i[5], 0, 0, 0))]
        + [by_block(3, *weights.shape[1:])],
        [
            jax.ShapeDtypeStruct((2, 512, ROWS), jnp.float32),
            jax.ShapeDtypeStruct((2, 512, ROWS), jnp.bfloat16),
            jax.ShapeDtypeStruct((4, 2, 1024, 384), jnp.bfloat16),
        ],
        [None, None, BY_STEP],
        [pltpu.VMEM((512, 8), jnp.float32)],
        2 * 1024 * 3072 * ROWS,
    )


def project_again(index, features, weights):
    return call(
        project_again_kernel,
        index,
        [features, weights],
        [BY_STEP, by_block(3, *weights.shape[1:])],
        PARTS,
        [None, None],
        SUMS,
        2 * 1024 * 3072 * ROWS,
    )


def attend_kernel(mine_ref, got_ref, q_gain_ref, k_gain_ref, out_ref):
    for frame in range(2):
        rows = slice(frame * PATCHES, (frame + 1) * PATCHES)
        for head in range(2):

            def part(which):
                cols = slice(which * 256 + head * HD, which * 256 + (head + 1) * HD)
                return mine_ref[rows, cols] + got_ref[rows, cols].astype(jnp.float32)

            queries = norm_rows(part(0), q_gain_ref[...]).astype(jnp.bfloat16)
            key_vecs = norm_rows(part(1), k_gain_ref[...]).astype(jnp.bfloat16)
            scores = lax.dot_general(
                queries, key_vecs, (((1,), (1,)), ((), ())), preferred_element_type=jnp.float32
            ) / math.sqrt(HD)
            exponent = jnp.exp(scores)
            probs = (exponent / jnp.sum(exponent, axis=-1, keepdims=True)).astype(jnp.bfloat16)
            out_ref[rows, head * HD : (head + 1) * HD] = jnp.dot(
                probs, part(2).astype(jnp.bfloat16), preferred_element_type=jnp.float32
            ).astype(jnp.bfloat16)


def attend(mine, got, q_gain, k_gain):
    return pl.pallas_call(
        attend_kernel,
        out_shape=jax.ShapeDtypeStruct((512, 256), jnp.bfloat16),
        compiler_params=pltpu.CompilerParams(vmem_limit_bytes=16 << 20),
        cost_estimate=pl.CostEstimate(
            flops=4 * 4 * 256 * 256 * 128, bytes_accessed=512 * 768 * 6, transcendentals=4 * 256 * 256
        ),
    )(mine, got, q_gain.reshape(1, HD), k_gain.reshape(1, HD))


def output_kernel(index, att_own, att_other, act_ref, w_down, *refs):
    w_out, w_rest, outs, w_ref = refs[:5], refs[5:9], refs[9:13], refs[13]
    step, first = pl.program_id(0), index[2] == 0
    for j in range(4):

        @pl.when(step == j)
        def _():
            if j == 3:
                w_ref[:128] = w_out[3][...]
                w_ref[128:256] = w_out[4][...]
            else:
                w_ref[:256] = w_out[j][...]
            w_ref[256:] = w_rest[j][...]

    own_first = index[1] == 0
    att = jnp.concatenate(
        [
            jnp.where(own_first, att_own[...], att_other[...]),
            jnp.where(own_first, att_other[...], att_own[...]),
        ]
    )
    act = act_ref[...].reshape(1024, ROWS)
    term = jnp.dot(act[:, :512], w_down[0], preferred_element_type=jnp.float32)
    mixed = jnp.concatenate([att, act[:, 512:]], axis=1)
    term += jnp.dot(mixed, w_ref[...], preferred_element_type=jnp.float32)
    term = term.astype(jnp.bfloat16)
    for block in range(2):
        part = term[block * 512 : (block + 1) * 512]
        outs[2 * block][0] = jnp.where(first, part[:, :384], part[:, 384:])
        outs[2 * block + 1][0] = jnp.where(first, part[:, 384:], part[:, :384])


def output_terms(index, att_own, att_other, activated, w_down, w_out, w_rest):
    out = jax.ShapeDtypeStruct((4, 512, 384), jnp.bfloat16)
    out_spec = pl.BlockSpec((1, 512, 384), lambda j, i: ((i[4] + order(j)) % 4, 0, 0))
    return call(
        output_kernel,
        index,
        [att_own, att_other, activated, w_down, *w_out, *w_rest],
        [None] * 3 + [by_block(0, 512, ROWS)] + [None] * 9,
        [out] * 4,
        [out_spec] * 4,
        [pltpu.VMEM((512, ROWS), jnp.bfloat16)],
        2 * 1024 * 1024 * 4 * ROWS,
        vmem=50 << 20,
    )


def after(value, *others):
    return lax.optimization_barrier((value, *others))[0]


def ring(block, axis, halves, ready=lambda *v: v):
    after, before = ready(shift(block, axis, -1), shift(block, axis, 1))
    return block, after, before, shift(halves(before)[0], axis, 1), shift(halves(after)[1], axis, -1)


def moments(piece):
    value = piece.astype(jnp.float32)
    mean = jnp.mean(value, axis=-1)
    return mean, jnp.sum((value - mean[..., None]) ** 2, axis=-1)


def merge(stats, count):
    means = [s[0] for s in stats]
    centre = 0.25 * (means[0] + means[1] + means[2] + means[3])
    total = stats[0][1] + stats[1][1] + stats[2][1] + stats[3][1]
    for m in means:
        total = total + count * (m - centre) ** 2
    return centre, total


def shards(tokens, ln_gain, w_qkv, q_gain, k_gain, w_up, w_out, w_down):
    y, x, h, l, c = (lax.axis_index(a) for a in ("y", "x", "h", "l", "c"))
    slot = jnp.where(l == h, 1, 0)
    index = jnp.stack([y, slot, c, x, (y - x + 4) % 4, l]).astype(jnp.int32)

    up_all = lax.all_gather(w_up[None], "y", axis=0)
    qkv_all = lax.all_gather(w_qkv.transpose(1, 0, 2), "y", axis=0)
    down_all = lax.all_gather(w_down[:512], "y", axis=0)

    block_a = move_z(tokens, [(1, 0), (0, 2), (3, 1), (2, 3)])
    block_b = move_z(tokens, [(0, 0), (1, 2), (2, 1), (3, 3)])
    out_near = shift(w_out, "y", -1), shift(w_out, "y", 1)
    own = ring(after(jnp.stack([block_a, block_b]), *out_near), "x", lambda v: (v[0], v[1]))
    other = [shift(piece, "c", 1) for piece in own]

    parts = [moments(piece) for piece in own]
    last = [jnp.stack([a, b]) for a, b in zip(parts[3], parts[4])]
    stats = jnp.stack(merge([*parts[:3], last], 384))
    cross = lax.ppermute(stats, ("l", "c"), [(i, 3 - i) for i in range(4)])
    centre, spread = merge([stats, shift(stats, "c", 1), shift(stats, "l", 1), cross], 1536)
    stats = jnp.concatenate([centre, lax.rsqrt(spread / 6144 + EPS), centre, centre])
    gain = ln_gain.reshape(4, 2, 2, 1, 384)

    up_sum, up_sent, features = project(
        index, own, other, stats, gain, up_all
    )
    out_near = after(out_near, up_sum)
    out_far = shift(out_near[1][:128], "y", 1), shift(out_near[0][128:], "y", -1)
    out_pieces = w_out, *out_near, *out_far
    qkv_all = after(qkv_all, *out_far)
    rest = after(w_down[512:], qkv_all)
    down_pieces = [rest] + [shift(rest, "y", -o) for o in STEPS[1:]]

    pre_act = up_sum + shift(up_sent, "l", 1).astype(jnp.float32)
    activated = jax.nn.gelu(pre_act, approximate=False).astype(jnp.bfloat16)

    qkv_mine, qkv_theirs = project_again(index, features, qkv_all)
    got = after(shift(qkv_theirs, "l", 1), activated)
    attended = attend(qkv_mine, got, q_gain, k_gain)
    attended_other = shift(attended, "l", 1)

    def start_sums(keep, got):
        pair = [keep[o].astype(jnp.float32) + got[o].astype(jnp.float32) for o in range(4)]
        far = pair[2].astype(jnp.bfloat16)
        return pair, shift(far[:256], "x", 1), shift(far[256:], "x", -1)

    def finish_sums(pair, first, second, pairs):
        f32 = lambda v: v.astype(jnp.float32)
        up = jnp.concatenate([pair[1][:256] + f32(first), pair[1][256:]]).astype(jnp.bfloat16)
        down = jnp.concatenate([pair[3][:256], pair[3][256:] + f32(second)]).astype(jnp.bfloat16)
        summed = pair[0] + f32(shift(up, "x", 1)) + f32(shift(down, "x", -1))
        return f32(move_z(summed.astype(jnp.bfloat16), pairs))

    keep_a, send_a, keep_b, send_b = output_terms(
        index, attended, attended_other, activated, down_all, out_pieces, down_pieces
    )
    sums_a = start_sums(keep_a, shift(send_a, "c", 1))
    sums_b = start_sums(keep_b, shift(send_b, "c", 1))
    part_a = finish_sums(*sums_a, [(0, 1), (2, 0), (1, 3), (3, 2)])
    part_b = finish_sums(*sums_b, [(0, 0), (2, 1), (1, 2), (3, 3)])
    return (tokens.astype(jnp.float32) + part_a + part_b).astype(jnp.bfloat16)


def solution(mesh):
    fine = Mesh(mesh.devices.reshape(4, 2, 4, 2, 2), AXES)
    row, col = ("y", "l"), ("x", "h", "c")
    in_specs = (
        P(row, col),
        P(),
        P(row, None, col),
        P(),
        P(),
        P(row, col),
        P(col, row),
        P(col, row),
    )
    return jax.shard_map(shards, mesh=fine, in_specs=in_specs, out_specs=P(row, col), check_vma=False)
```
